32 devices in a mesh: ctx: 8 (over z, core), head: 4 (over y, x).
Axes of the slice: x: 2, y: 2, z: 4, core: 2. Of those that a mesh axis runs over, the one named last changes fastest.
Arguments:
- query_rows: bfloat16 [8192, 512], P('ctx', 'head'), may hold values from -0.5 to 0.5
- key_rows: bfloat16 [8192, 512], P('ctx', 'head'), may hold values from -0.5 to 0.5
- value_rows: bfloat16 [8192, 512], P('ctx', 'head'), may hold values from -40 to 40, as said below
- gate_logits: bfloat16 [8192, 512], P('ctx', 'head'), may hold values from -8 to 8
- log_decay: float32 [8192, 4], P('ctx', 'head'), may hold values from -1.2 to 0, as said below
- norm_gain: float32 [512], P('head'), may hold values from 0.1 to 1.9
- state_in: float32 [4, 128, 128], P('head'), may hold values from -256 to 256
- cotangent: bfloat16 [8192, 512], P('ctx', 'head'), may hold values from -6 to 6
- regroup: int32 [64], replicated, may hold values from 0 to 63, as said below
Outputs:
- gated_out: bfloat16 [8192, 512], P('ctx', 'head')
- grad_query: bfloat16 [8192, 512], P('ctx', 'head')
- grad_key: bfloat16 [8192, 512], P('ctx', 'head')
- grad_value: bfloat16 [8192, 512], P('ctx', 'head')
- grad_gate: bfloat16 [8192, 512], P('ctx', 'head')
The draws below stay inside these ranges and needn't reach their ends.
Inputs may be any that keep to these rules, and one draw needn't show every extreme that they name: `value_rows`: values of order one per entry times a column and a row factor. `log_decay`: never positive. `regroup`: a permutation of the 64 pieces; the 8 places held by one device's 1024 tokens take exactly one piece from each device's 1024 tokens.
All inputs are finite; a program needn't handle non-finite values.
Results may differ from the reference program's by a relative error of at most 0.012.
Values may be sent and summed in bfloat16 or wider, within the bound.
A program may use at most 64 MiB of HBM per device.

```python
import jax
import jax.numpy as jnp
from jax import lax

HD = 128
TOK_DEV = 1024
BLOCK = 1024
HEADS = 4
WIDTH = 512
TOKENS = 8192
PEERS = 8
PIECES = 64
PIECE = 128


def draw_value_rows(key, part):
    key_base = jax.random.fold_in(key, 11)
    key_jitter = jax.random.fold_in(key, 12)
    key_row = jax.random.fold_in(key, 13)
    column = jnp.arange(WIDTH, dtype=jnp.float32) / float(WIDTH - 1)
    random_noise = jax.random.uniform(key_jitter, (WIDTH,), minval=-0.1, maxval=0.1)
    power = jnp.clip(column + random_noise, 0.0, 1.0)
    row_scale = jnp.exp(jax.random.uniform(key_row, (TOKENS, 1), minval=jnp.log(0.5), maxval=jnp.log(2.0)))
    base = jnp.clip(jax.random.normal(key_base, (TOKENS, WIDTH)), -6.0, 6.0)
    values = 0.3 * base * row_scale * jnp.power(10.0, power)[None, :]
    return values.astype(jnp.bfloat16)


def draw_log_decay(key, part):
    key_kind = jax.random.fold_in(key, 21)
    key_fast = jax.random.fold_in(key, 22)
    key_slow = jax.random.fold_in(key, 23)
    key_device = jax.random.fold_in(key, 24)
    key_place = jax.random.fold_in(key, 25)
    key_spots = jax.random.fold_in(key, 26)
    key_depth = jax.random.fold_in(key, 27)
    share = 0.5
    fast = jax.random.uniform(key_kind, (HEADS,)) < share
    fast_rate = jax.random.uniform(key_fast, (HEADS,), minval=1.0 / 50.0, maxval=1.0 / 30.0)
    slow_rate = jnp.exp(jax.random.uniform(key_slow, (HEADS,), minval=jnp.log(0.05 / TOKENS), maxval=jnp.log(0.5 / TOKENS)))
    reference_fading_speed = jnp.where(fast, fast_rate, slow_rate)
    accelerator_scaling = jnp.exp(jax.random.uniform(key_device, (TOKENS // TOK_DEV, HEADS), minval=jnp.log(0.5), maxval=jnp.log(2.0)))
    accelerator_scaling = jnp.repeat(accelerator_scaling, TOK_DEV, axis=0)
    position_slot_scaling = jnp.exp(jax.random.uniform(key_place, (TOKENS, HEADS), minval=jnp.log(0.5), maxval=jnp.log(2.0)))
    spots = jax.random.randint(key_spots, (2,), 0, TOKENS)
    stack_level_number = jax.random.uniform(key_depth, (2, HEADS), minval=0.22, maxval=0.45)
    agreement_tallies = (jnp.arange(TOKENS)[:, None] == spots[None, :]).astype(jnp.float32)
    sudden_spike_tally = jnp.sum(agreement_tallies[:, :, None] * stack_level_number[None, :, :], axis=1)
    return (-(reference_fading_speed[None, :] * accelerator_scaling * position_slot_scaling) - sudden_spike_tally).astype(jnp.float32)


def shuffled(one_key):
    return jax.random.permutation(one_key, PEERS)


def draw_regroup(key, part):
    dest_keys = jax.random.split(jax.random.fold_in(key, 31), PEERS)
    source_keys = jax.random.split(jax.random.fold_in(key, 32), PEERS)
    sources = jax.vmap(shuffled)(dest_keys)
    local_pick = jax.vmap(shuffled)(source_keys)
    local = local_pick[sources, jnp.arange(PEERS)[:, None]]
    return (sources * PEERS + local).reshape((PIECES,)).astype(jnp.int32)


def block_scale(own_key, extent, cuts, smallest, largest):
    def one(dim, parts):
        draws = jax.random.uniform(jax.random.fold_in(jax.random.fold_in(own_key, 6), dim), (parts,), jnp.float32, smallest / len(cuts), largest / len(cuts))
        return jnp.repeat(jnp.exp(draws), extent[dim] // parts).reshape((-1,) + (1,) * (len(extent) - dim - 1))

    gain = one(*cuts[0])
    for cut in cuts[1:]:
        gain = gain * one(*cut)
    return gain


def noise(stream_key, shape, width, bound, cuts=(), kind=jnp.bfloat16):
    loudness = block_scale(stream_key, shape, cuts, -0.22, 0.18) if cuts else 1.0
    entries = jax.random.normal(stream_key, shape, jnp.float32) * width * loudness
    return jnp.minimum(jnp.maximum(entries, -bound), bound).astype(kind)


def setup_inputs(seed: int = 0) -> dict:
    key_list = jax.random.split(jax.random.key(seed), 10)
    return {
        "query_rows": noise(key_list[0], (TOKENS, WIDTH), 0.08, 0.5, ((0, 8), (1, 4))),
        "key_rows": noise(key_list[1], (TOKENS, WIDTH), 0.08, 0.5, ((0, 8), (1, 4))),
        "value_rows": draw_value_rows(jax.random.fold_in(key_list[9], 71), 0),
        "gate_logits": noise(key_list[3], (TOKENS, WIDTH), 1.5, 8.0, ((0, 8), (1, 4))),
        "log_decay": draw_log_decay(jax.random.fold_in(key_list[9], 71), 0),
        "norm_gain": jnp.clip(1.0 + 0.18 * jax.random.normal(key_list[5], (WIDTH,), jnp.float32), 0.1, 1.9),
        "state_in": noise(key_list[6], (HEADS, HD, HD), 40.0, 256.0, ((0, 4),), jnp.float32),
        "cotangent": noise(key_list[7], (TOKENS, WIDTH), 1.0, 6.0, ((0, 8), (1, 4))),
        "regroup": draw_regroup(jax.random.fold_in(key_list[9], 71), 0),
    }


exact_mode = lax.Precision.HIGHEST

def block_masks(query_blk, key_blk, decay_blk):
    count = query_blk.shape[0]
    cum_log = jnp.cumsum(decay_blk, axis=0)
    positions = jnp.arange(count)
    causal = positions[:, None] >= positions[None, :]
    head_log = cum_log.T
    spread = jnp.where(causal[None], head_log[:, :, None] - head_log[:, None, :], 0.0)
    decay_mask = jnp.where(causal[None], jnp.exp(spread), 0.0)
    scores = jnp.einsum('thd,jhd->htj', query_blk.astype(jnp.float32), key_blk.astype(jnp.float32))
    attn_probs = (scores * decay_mask).astype(jnp.bfloat16)
    return (cum_log, decay_mask, attn_probs)

def block_forward(kv_state, inputs):
    query_blk, key_blk, value_blk, decay_blk = inputs
    cum_log, decay_mask, attn_probs = block_masks(query_blk, key_blk, decay_blk)
    within = jnp.einsum('htj,jhd->thd', attn_probs.astype(jnp.float32), value_blk.astype(jnp.float32))
    carried = jnp.exp(cum_log)[:, :, None] * jnp.einsum('thd,hde->the', query_blk.astype(jnp.float32), kv_state, precision=exact_mode)
    block_total = cum_log[-1]
    tail_weight = jnp.exp(block_total[None, :] - cum_log)
    update = jnp.einsum('thd,the->hde', key_blk.astype(jnp.float32) * tail_weight[:, :, None], value_blk.astype(jnp.float32), precision=exact_mode)
    next_state = jnp.exp(block_total)[:, None, None] * kv_state + update
    return (next_state, (within + carried, kv_state))

def block_backward(grad_state, inputs):
    query_blk, key_blk, value_blk, grad_blk, decay_blk, kv_state = inputs
    cum_log, decay_mask, attn_probs = block_masks(query_blk, key_blk, decay_blk)
    block_total = cum_log[-1]
    tail_weight = jnp.exp(block_total[None, :] - cum_log)[:, :, None]
    rise = jnp.exp(cum_log)[:, :, None]
    query_wide = query_blk.astype(jnp.float32)
    key_wide = key_blk.astype(jnp.float32)
    value_wide = value_blk.astype(jnp.float32)
    broad_derivative_matrix = grad_blk.astype(jnp.float32)
    grad_scores = jnp.einsum('thd,jhd->htj', broad_derivative_matrix, value_wide)
    score_grad = (grad_scores * decay_mask).astype(jnp.bfloat16).astype(jnp.float32)
    grad_q = jnp.einsum('htj,jhd->thd', score_grad, key_wide) + rise * jnp.einsum('the,hde->thd', broad_derivative_matrix, kv_state, precision=exact_mode)
    grad_k = jnp.einsum('htj,thd->jhd', score_grad, query_wide) + tail_weight * jnp.einsum('the,hde->thd', value_wide, grad_state, precision=exact_mode)
    grad_v = jnp.einsum('htj,thd->jhd', attn_probs.astype(jnp.float32), broad_derivative_matrix) + tail_weight * jnp.einsum('thd,hde->the', key_wide, grad_state, precision=exact_mode)
    prior = jnp.exp(block_total)[:, None, None] * grad_state + jnp.einsum('thd,the->hde', query_wide * rise, broad_derivative_matrix, precision=exact_mode)
    return (prior, (grad_q, grad_k, grad_v))

def reference(query_rows, key_rows, value_rows, gate_logits, log_decay, norm_gain, state_in, cotangent, regroup):
    blocks = TOKENS // BLOCK

    def divided_segments(array):
        return array.reshape((blocks, BLOCK, HEADS, HD))
    query_b = divided_segments(query_rows)
    key_b = divided_segments(key_rows)
    value_b = divided_segments(value_rows)
    decay_b = log_decay.reshape((blocks, BLOCK, HEADS))
    forward = lax.scan(block_forward, state_in, (query_b, key_b, value_b, decay_b))
    attended, starts = forward[1]
    flat = attended.reshape((TOKENS, WIDTH))
    gate_on = jax.nn.sigmoid(gate_logits.astype(jnp.float32))
    inv_rms = lax.rsqrt(lax.optimization_barrier(jnp.sum(flat * flat, axis=1)) / WIDTH + 1e-06)
    normed = flat * inv_rms[:, None] * norm_gain[None, :]
    gated = (normed * gate_on).astype(jnp.bfloat16)
    gated_out = gated.reshape((PIECES, PIECE, WIDTH))[regroup].reshape((TOKENS, WIDTH))
    broad_derivative_matrix = cotangent.astype(jnp.float32)
    grad_gate = (broad_derivative_matrix * normed * gate_on * (1.0 - gate_on)).astype(jnp.bfloat16)
    scaled_grad = broad_derivative_matrix * gate_on * norm_gain[None, :]
    cross = lax.optimization_barrier(jnp.sum(scaled_grad * flat, axis=1))
    cube = inv_rms * inv_rms * inv_rms
    grad_attended = (inv_rms[:, None] * scaled_grad - flat * (cube * cross / WIDTH)[:, None]).astype(jnp.bfloat16)
    zero_state = jnp.zeros((HEADS, HD, HD), jnp.float32)
    backward = lax.scan(block_backward, zero_state, (query_b, key_b, value_b, divided_segments(grad_attended), decay_b, starts), reverse=True)
    grad_q, grad_k, grad_v = backward[1]
    grad_query = grad_q.reshape((TOKENS, WIDTH)).astype(jnp.bfloat16)
    grad_key = grad_k.reshape((TOKENS, WIDTH)).astype(jnp.bfloat16)
    grad_value = grad_v.reshape((TOKENS, WIDTH)).astype(jnp.bfloat16)
    return (gated_out, grad_query, grad_key, grad_value, grad_gate)
```

```python
import functools

import jax
import jax.numpy as jnp
from jax import lax
from jax.experimental import pallas as pl
from jax.experimental.pallas import tpu as pltpu
from jax.sharding import PartitionSpec as P

F32 = jnp.float32
BF16 = jnp.bfloat16
MESH = pl.DeviceIdType.MESH
T = 128
NT = (((1,), (1,)), ((), ()))
NN = (((1,), (0,)), ((), ()))
TN = (((0,), (0,)), ((), ()))


def dot(a, b, dims):
    return lax.dot_general(a, b, dims, preferred_element_type=F32)


def kernel(
    n, m, rows,
    q_hbm, k_hbm, v_hbm, gate_hbm, ct_hbm, decay_ref, gain_ref, state_ref, regroup,
    go_out, gq_out, gk_out, gv_out, gg_out,
    q, k, v, gate, ct,
    cum_b, rise_b, tail_b, mask, probs, att, scaled, gated, grad, qr, gk_acc, gv_acc,
    go, gq, gk, gv, gg,
    tots, swap_out, swap_in, f_out, f_in, b_out, b_in, stat, a_out, a_in, start_state,
    in_sem, out_sem, tot_send, tot_recv, swap_send, swap_recv,
    f_send, f_recv, b_send, b_recv, h_send, h_recv, a_send, a_recv,
):
    me = lax.axis_index("ctx")
    head = lax.axis_index("head")
    chip = me // 2
    core = me % 2
    mate = me + 1 - 2 * core
    chips = n // 2
    nb = rows // T
    piece = rows // n
    width_all = m * T
    shift = n.bit_length() - 1

    loads = [
        pltpu.make_async_copy(src, dst, in_sem.at[i])
        for i, (src, dst) in enumerate(
            [(k_hbm, k), (v_hbm, v), (q_hbm, q), (gate_hbm, gate), (ct_hbm, ct)]
        )
    ]
    for load in loads:
        load.start()

    barrier = pltpu.get_barrier_semaphore()

    def greet_ctx(o, c):
        pl.semaphore_signal(
            barrier, inc=1, device_id={"ctx": lax.rem(me + o, n)}, device_id_type=MESH
        )
        return c

    def greet_head(o, c):
        pl.semaphore_signal(
            barrier, inc=1, device_id={"head": lax.rem(head + o, m)}, device_id_type=MESH
        )
        return c

    lax.fori_loop(1, n, greet_ctx, 0)
    lax.fori_loop(1, m, greet_head, 0)

    row_i = lax.broadcasted_iota(jnp.int32, (T, T), 0)
    col_i = lax.broadcasted_iota(jnp.int32, (T, T), 1)
    upper = (row_i <= col_i).astype(F32)
    partial_sums = lax.dot_general(
        decay_ref[...], upper, NN, precision=lax.Precision.HIGHEST, preferred_element_type=F32
    )
    crow = []
    offset = jnp.zeros((1, 1), F32)
    for r in range(nb):
        row = partial_sums[r : r + 1, :]
        crow.append(row + offset)
        offset = offset + row[:, T - 1 : T]
    total = jnp.broadcast_to(crow[-1][:, T - 1 : T], (1, T))
    tots[pl.ds(me, 1)] = jnp.broadcast_to(total, (8, T))[None]
    for r in range(nb):
        sl = slice(r * T, (r + 1) * T)
        cb = jnp.transpose(jnp.broadcast_to(crow[r], (T, T)))
        cum_b[sl, :] = cb
        rise_b[sl, :] = jnp.exp(cb)
        tail_b[sl, :] = jnp.exp(total - cb)

    loads[0].wait()
    loads[1].wait()
    weighted = (k[...].astype(F32) * tail_b[...]).astype(BF16)
    local = dot(weighted, v[...], TN)
    swap_out[0] = local

    pl.semaphore_wait(barrier, n - 1 + m - 1)

    def swap_copy(i):
        return pltpu.make_async_remote_copy(
            src_ref=swap_out.at[i], dst_ref=swap_in.at[i],
            send_sem=swap_send.at[i], recv_sem=swap_recv.at[i],
            device_id={"ctx": mate}, device_id_type=MESH,
        )

    swap_copy(0).start()

    def tot_copy(slot, to):
        return pltpu.make_async_remote_copy(
            src_ref=tots.at[me], dst_ref=tots.at[slot],
            send_sem=tot_send.at[to], recv_sem=tot_recv.at[slot],
            device_id={"ctx": to}, device_id_type=MESH,
        )

    def tot_go(o, c):
        tot_copy(me, lax.rem(me + o, n)).start()
        return c

    lax.fori_loop(1, n, tot_go, 0)

    loads[2].wait()
    causal = row_i >= col_i

    def decay_tile(a, b):
        diff = cum_b[a * T : (a + 1) * T, :] - crow[b]
        if a == b:
            return jnp.where(causal, jnp.exp(jnp.where(causal, diff, 0.0)), 0.0)
        return jnp.exp(diff)

    def scores_for(a):
        w = (a + 1) * T
        s = dot(q[a * T : w, :], k[:w, :], NT)
        for b in range(a + 1):
            d = decay_tile(a, b)
            mask[a * T : w, b * T : (b + 1) * T] = d
            probs[a * T : w, b * T : (b + 1) * T] = (s[:, b * T : (b + 1) * T] * d).astype(BF16)

    half = nb // 4
    for a in range(half):
        scores_for(a)

    def tot_wait(o, c):
        tot_copy(lax.rem(me + o, n), lax.rem(me + o, n)).wait_recv()
        return c

    lax.fori_loop(1, n, tot_wait, 0)
    swap_copy(0).wait_recv()

    def tot_row(i):
        return tots[pl.ds(i, 1)][0, 0:1, :]

    mine, other = swap_out[0], swap_in[0]
    is_late = core == 1
    later = jnp.exp(jnp.where(is_late, total, tot_row(mate)))
    f_out[...] = (later * jnp.where(is_late, other, mine) + jnp.where(is_late, mine, other)).astype(BF16)

    def f_copy(slot, to):
        return pltpu.make_async_remote_copy(
            src_ref=f_out, dst_ref=f_in.at[slot],
            send_sem=f_send.at[to], recv_sem=f_recv.at[slot],
            device_id={"ctx": 2 * to + core}, device_id_type=MESH,
        )

    def f_go(to, c):
        f_copy(chip, to).start()
        return c

    lax.fori_loop(chip + 1, chips, f_go, 0)

    for a in range(half, nb):
        scores_for(a)
    for a in range(nb):
        w = (a + 1) * T
        att[a * T : w, :] = dot(probs[a * T : w, :w], v[:w, :], NN)
    qr[...] = (q[...].astype(F32) * rise_b[...]).astype(BF16)
    loads[3].wait()
    loads[4].wait()
    on = jax.nn.sigmoid(gate[...].astype(F32))
    scaled[...] = ct[...].astype(F32) * on * gain_ref[...]

    def chip_total(i):
        return tot_row(2 * i) + tot_row(2 * i + 1)

    def f_join(i, state):
        f_copy(i, i).wait_recv()
        return jnp.exp(chip_total(i)) * state + f_in[pl.ds(i, 1)][0].astype(F32)

    state = lax.fori_loop(0, chip, f_join, state_ref[0])
    state = jnp.where(is_late, jnp.exp(tot_row(mate)) * state + other, state)
    start_state[...] = state.astype(BF16)

    for r in range(nb):
        sl = slice(r * T, (r + 1) * T)
        flat = att[sl, :] + rise_b[sl, :] * dot(q[sl, :], start_state[...], NN)
        att[sl, :] = flat
        stat[pl.ds(head, 1), r : r + 1, :] = jnp.sum(
            jnp.transpose(flat * flat), axis=0, keepdims=True
        )[None]
        stat[pl.ds(head, 1), nb + r : nb + r + 1, :] = jnp.sum(
            jnp.transpose(flat * scaled[sl, :]), axis=0, keepdims=True
        )[None]

    def h_copy(slot, to):
        return pltpu.make_async_remote_copy(
            src_ref=stat.at[head], dst_ref=stat.at[slot],
            send_sem=h_send.at[to], recv_sem=h_recv.at[slot],
            device_id={"head": to}, device_id_type=MESH,
        )

    def h_go(o, c):
        h_copy(head, lax.rem(head + o, m)).start()
        return c

    lax.fori_loop(1, m, h_go, 0)

    def h_join(o, acc):
        i = lax.rem(head + o, m)
        h_copy(i, i).wait_recv()
        return acc + stat[pl.ds(i, 1)][0]

    sums = lax.fori_loop(1, m, h_join, stat[pl.ds(head, 1)][0])
    inv = lax.rsqrt(sums[:nb] / width_all + 1e-06)
    coef = inv * inv * inv * sums[nb:] / width_all
    for r in range(nb):
        sl = slice(r * T, (r + 1) * T)
        inv_b = jnp.transpose(jnp.broadcast_to(inv[r : r + 1, :], (T, T)))
        coef_b = jnp.transpose(jnp.broadcast_to(coef[r : r + 1, :], (T, T)))
        flat = att[sl, :]
        grad[sl, :] = (inv_b * scaled[sl, :] - flat * coef_b).astype(BF16)
        att[sl, :] = flat * inv_b * gain_ref[...]

    back = dot(qr[...], grad[...], TN)
    swap_out[1] = back
    swap_copy(1).start()

    for r in range(nb):
        sl = slice(r * T, (r + 1) * T)
        on = jax.nn.sigmoid(gate[sl, :].astype(F32))
        normed = att[sl, :]
        out = (normed * on).astype(BF16)
        for part in range(T // piece):
            gated[r * (T // piece) + part] = out[part * piece : (part + 1) * piece]
        gg[sl, :] = (ct[sl, :].astype(F32) * normed * on * (1.0 - on)).astype(BF16)

    swap_copy(1).wait_recv()
    mine_b, other_b = swap_out[1], swap_in[1]
    earlier = jnp.exp(jnp.where(is_late, tot_row(mate), total))
    b_out[...] = (
        earlier * jnp.where(is_late, mine_b, other_b) + jnp.where(is_late, other_b, mine_b)
    ).astype(BF16)

    def b_copy(slot, to):
        return pltpu.make_async_remote_copy(
            src_ref=b_out, dst_ref=b_in.at[slot],
            send_sem=b_send.at[to], recv_sem=b_recv.at[slot],
            device_id={"ctx": 2 * to + core}, device_id_type=MESH,
        )

    def b_go(to, c):
        b_copy(chip, to).start()
        return c

    lax.fori_loop(0, chip, b_go, 0)

    def pick(d):
        def one(s, found):
            p = regroup[d * n + s]
            apart = lax.shift_right_logical(p, shift) - me
            return found + (1 - jnp.minimum(apart * apart, 1)) * (p & (n - 1))

        return lax.fori_loop(0, n, one, jnp.int32(0), unroll=8)

    def wanted(d):
        return gated[pick(d)]

    def a_copy(slot, to):
        return pltpu.make_async_remote_copy(
            src_ref=a_out.at[to], dst_ref=a_in.at[slot],
            send_sem=a_send.at[to], recv_sem=a_recv.at[slot],
            device_id={"ctx": to}, device_id_type=MESH,
        )

    def a_go(o, c):
        to = lax.rem(me + o, n)
        a_out[to] = wanted(to)
        a_copy(me, to).start()
        return c

    lax.fori_loop(1, n, a_go, 0)
    a_in[me] = wanted(me)

    stores = [
        pltpu.make_async_copy(src, dst, out_sem.at[i])
        for i, (src, dst) in enumerate(
            [(go, go_out), (gq, gq_out), (gk, gk_out), (gv, gv_out), (gg, gg_out)]
        )
    ]
    stores[4].start()

    for a in range(nb):
        w = (a + 1) * T
        sl = slice(a * T, w)
        ds = (dot(grad[sl, :], v[:w, :], NT) * mask[sl, :w]).astype(BF16)
        gq[sl, :] = (
            dot(ds, k[:w, :], NN) + rise_b[sl, :] * dot(grad[sl, :], start_state[...], NT)
        ).astype(BF16)
        dk = dot(ds, q[sl, :], TN)
        dv = dot(probs[sl, :w], grad[sl, :], TN)
        if a:
            gk_acc[: a * T, :] += dk[: a * T]
            gv_acc[: a * T, :] += dv[: a * T]
        gk_acc[sl, :] = dk[a * T :]
        gv_acc[sl, :] = dv[a * T :]
    stores[1].start()

    def b_join(o, state):
        i = chips - 1 - o
        b_copy(i, i).wait_recv()
        return jnp.exp(chip_total(i)) * state + b_in[pl.ds(i, 1)][0].astype(F32)

    after = lax.fori_loop(0, chips - 1 - chip, b_join, jnp.zeros((T, T), F32))
    after = jnp.where(is_late, after, jnp.exp(tot_row(mate)) * after + other_b).astype(BF16)
    gk[...] = (gk_acc[...] + tail_b[...] * dot(v[...], after, NT)).astype(BF16)
    stores[2].start()
    gv[...] = (gv_acc[...] + tail_b[...] * dot(k[...], after, NN)).astype(BF16)
    stores[3].start()

    def a_wait(o, c):
        i = lax.rem(me + o, n)
        a_copy(i, i).wait_recv()
        return c

    lax.fori_loop(1, n, a_wait, 0)
    for s in range(n):
        src = lax.shift_right_logical(regroup[me * n + s], shift)
        go[s * piece : (s + 1) * piece, :] = a_in[src]
    stores[0].start()

    swap_copy(0).wait_send()
    swap_copy(1).wait_send()

    def end_ctx(o, c):
        to = lax.rem(me + o, n)
        tot_copy(to, to).wait_send()
        a_copy(to, to).wait_send()
        return c

    lax.fori_loop(1, n, end_ctx, 0)

    def end_head(o, c):
        to = lax.rem(head + o, m)
        h_copy(to, to).wait_send()
        return c

    lax.fori_loop(1, m, end_head, 0)

    def end_f(to, c):
        f_copy(to, to).wait_send()
        return c

    lax.fori_loop(chip + 1, chips, end_f, 0)

    def end_b(to, c):
        b_copy(to, to).wait_send()
        return c

    lax.fori_loop(0, chip, end_b, 0)
    for store in stores:
        store.wait()


def per_device(n, m, query, key, value, gate, decay, gain, state_in, cotangent, regroup):
    rows = query.shape[0]
    chips = n // 2
    nb = rows // T
    piece = rows // n
    big = lambda kind: pltpu.VMEM((rows, T), kind)
    dma = pltpu.SemaphoreType.DMA
    hbm = pl.BlockSpec(memory_space=pl.ANY)
    vmem = pl.BlockSpec(memory_space=pltpu.VMEM)
    smem = pl.BlockSpec(memory_space=pltpu.SMEM)
    return pl.pallas_call(
        functools.partial(kernel, n, m, rows),
        out_shape=[jax.ShapeDtypeStruct((rows, T), BF16)] * 5,
        in_specs=[hbm] * 5 + [vmem] * 3 + [smem],
        out_specs=[hbm] * 5,
        scratch_shapes=[big(BF16)] * 5
        + [big(F32)] * 3
        + [
            pltpu.VMEM((rows, rows), F32),
            pltpu.VMEM((rows, rows), BF16),
            big(F32), big(F32), pltpu.VMEM((n, piece, T), BF16), big(BF16), big(BF16), big(F32), big(F32),
        ]
        + [big(BF16)] * 5
        + [
            pltpu.VMEM((n, 8, T), F32),
            pltpu.VMEM((2, T, T), F32),
            pltpu.VMEM((2, T, T), F32),
            pltpu.VMEM((T, T), BF16),
            pltpu.VMEM((chips, T, T), BF16),
            pltpu.VMEM((T, T), BF16),
            pltpu.VMEM((chips, T, T), BF16),
            pltpu.VMEM((m, 2 * nb, T), F32),
            pltpu.VMEM((n, piece, T), BF16),
            pltpu.VMEM((n, piece, T), BF16),
            pltpu.VMEM((T, T), BF16),
        ]
        + [
            dma((5,)), dma((5,)), dma((n,)), dma((n,)), dma((2,)), dma((2,)),
            dma((chips,)), dma((chips,)), dma((chips,)), dma((chips,)),
            dma((m,)), dma((m,)), dma((n,)), dma((n,)),
        ],
        compiler_params=pltpu.CompilerParams(
            collective_id=0, has_side_effects=True, vmem_limit_bytes=62 << 20
        ),
        name="layer",
    )(
        query, key, value, gate, cotangent,
        decay.reshape((nb, T)), gain.reshape((1, T)), state_in, regroup,
    )


def solution(mesh):
    rows = P("ctx", "head")
    in_specs = (rows, rows, rows, rows, rows, P("head"), P("head", None, None), rows, P())
    body = functools.partial(per_device, mesh.shape["ctx"], mesh.shape["head"])
    return jax.shard_map(
        body, mesh=mesh, in_specs=in_specs, out_specs=(rows,) * 5, check_vma=False
    )
```

```python
import functools

import jax
import jax.numpy as jnp
from jax import lax
from jax.experimental import pallas as pl
from jax.experimental.pallas import tpu as pltpu
from jax.sharding import PartitionSpec as P

F32 = jnp.float32
BF16 = jnp.bfloat16
MESH = pl.DeviceIdType.MESH
T = 128
NT = (((1,), (1,)), ((), ()))
NN = (((1,), (0,)), ((), ()))
TN = (((0,), (0,)), ((), ()))


def dot(a, b, dims):
    return lax.dot_general(a, b, dims, preferred_element_type=F32)


def kernel(
    n, m, rows,
    q_hbm, k_hbm, v_hbm, gate_hbm, ct_hbm, decay_hbm, gain_hbm, state_hbm, regroup_hbm,
    go, gq, gk, gv, gg,
    q, k, v, gate, ct, decay_ref, gain_ref, state_ref, regroup,
    cum_b, rise_b, tail_b, mask, probs, att, scaled, gated, grad, qr, gk_acc, gv_acc,
    tots, swap_out, swap_in, f_out, f_in, b_out, b_in, stat, a_out, a_in, start_state,
    in_sem, tot_send, tot_recv, swap_send, swap_recv,
    f_send, f_recv, b_send, b_recv, h_send, h_recv, a_send, a_recv,
):
    me = lax.axis_index("ctx")
    head = lax.axis_index("head")
    chip = me // 2
    core = me % 2
    mate = me + 1 - 2 * core
    chips = n // 2
    nb = rows // T
    piece = rows // n
    width_all = m * T
    shift = n.bit_length() - 1

    loads = [
        pltpu.make_async_copy(src, dst, in_sem.at[i])
        for i, (src, dst) in enumerate(
            [
                (k_hbm, k), (v_hbm, v), (q_hbm, q), (gate_hbm, gate), (ct_hbm, ct),
                (decay_hbm, decay_ref), (gain_hbm, gain_ref), (state_hbm, state_ref),
                (regroup_hbm, regroup),
            ]
        )
    ]
    for i in (5, 0, 1, 2, 3, 4, 6, 7, 8):
        loads[i].start()

    barrier = pltpu.get_barrier_semaphore()

    def greet_ctx(o, c):
        pl.semaphore_signal(
            barrier, inc=1, device_id={"ctx": lax.rem(me + o, n)}, device_id_type=MESH
        )
        return c

    def greet_head(o, c):
        pl.semaphore_signal(
            barrier, inc=1, device_id={"head": lax.rem(head + o, m)}, device_id_type=MESH
        )
        return c

    lax.fori_loop(1, n, greet_ctx, 0)
    lax.fori_loop(1, m, greet_head, 0)

    row_i = lax.broadcasted_iota(jnp.int32, (T, T), 0)
    col_i = lax.broadcasted_iota(jnp.int32, (T, T), 1)
    upper = (row_i <= col_i).astype(F32)
    loads[5].wait()
    partial_sums = lax.dot_general(
        decay_ref[...], upper, NN, precision=lax.Precision.HIGHEST, preferred_element_type=F32
    )
    crow = []
    offset = jnp.zeros((1, 1), F32)
    for r in range(nb):
        row = partial_sums[r : r + 1, :]
        crow.append(row + offset)
        offset = offset + row[:, T - 1 : T]
    total = jnp.broadcast_to(crow[-1][:, T - 1 : T], (1, T))
    tots[pl.ds(me, 1)] = jnp.broadcast_to(total, (8, T))[None]
    for r in range(nb):
        sl = slice(r * T, (r + 1) * T)
        cb = jnp.transpose(jnp.broadcast_to(crow[r], (T, T)))
        cum_b[sl, :] = cb
        rise_b[sl, :] = jnp.exp(cb)
        tail_b[sl, :] = jnp.exp(total - cb)

    loads[0].wait()
    loads[1].wait()
    weighted = (k[...].astype(F32) * tail_b[...]).astype(BF16)
    local = dot(weighted, v[...], TN)
    swap_out[0] = local

    pl.semaphore_wait(barrier, n - 1 + m - 1)

    def swap_copy(i):
        return pltpu.make_async_remote_copy(
            src_ref=swap_out.at[i], dst_ref=swap_in.at[i],
            send_sem=swap_send.at[i], recv_sem=swap_recv.at[i],
            device_id={"ctx": mate}, device_id_type=MESH,
        )

    swap_copy(0).start()

    def tot_copy(slot, to):
        return pltpu.make_async_remote_copy(
            src_ref=tots.at[me], dst_ref=tots.at[slot],
            send_sem=tot_send.at[to], recv_sem=tot_recv.at[slot],
            device_id={"ctx": to}, device_id_type=MESH,
        )

    def tot_go(o, c):
        tot_copy(me, lax.rem(me + o, n)).start()
        return c

    lax.fori_loop(1, n, tot_go, 0)

    loads[2].wait()
    causal = row_i >= col_i

    def decay_tile(a, b):
        diff = cum_b[a * T : (a + 1) * T, :] - crow[b]
        if a == b:
            return jnp.where(causal, jnp.exp(jnp.where(causal, diff, 0.0)), 0.0)
        return jnp.exp(diff)

    def scores_for(a):
        w = (a + 1) * T
        s = dot(q[a * T : w, :], k[:w, :], NT)
        for b in range(a + 1):
            d = decay_tile(a, b)
            mask[a * T : w, b * T : (b + 1) * T] = d
            probs[a * T : w, b * T : (b + 1) * T] = (s[:, b * T : (b + 1) * T] * d).astype(BF16)

    half = nb // 4
    for a in range(half):
        scores_for(a)

    def tot_wait(o, c):
        tot_copy(lax.rem(me + o, n), lax.rem(me + o, n)).wait_recv()
        return c

    lax.fori_loop(1, n, tot_wait, 0)
    swap_copy(0).wait_recv()

    def tot_row(i):
        return tots[pl.ds(i, 1)][0, 0:1, :]

    mine, other = swap_out[0], swap_in[0]
    is_late = core == 1
    later = jnp.exp(jnp.where(is_late, total, tot_row(mate)))
    f_out[...] = (later * jnp.where(is_late, other, mine) + jnp.where(is_late, mine, other)).astype(BF16)

    def f_copy(slot, to):
        return pltpu.make_async_remote_copy(
            src_ref=f_out, dst_ref=f_in.at[slot],
            send_sem=f_send.at[to], recv_sem=f_recv.at[slot],
            device_id={"ctx": 2 * to + core}, device_id_type=MESH,
        )

    def f_go(to, c):
        f_copy(chip, to).start()
        return c

    lax.fori_loop(chip + 1, chips, f_go, 0)

    for a in range(half, nb):
        scores_for(a)
    for a in range(nb):
        w = (a + 1) * T
        att[a * T : w, :] = dot(probs[a * T : w, :w], v[:w, :], NN)
    qr[...] = (q[...].astype(F32) * rise_b[...]).astype(BF16)
    loads[3].wait()
    for i in (4, 6, 7, 8):
        loads[i].wait()
    on = jax.nn.sigmoid(gate[...].astype(F32))
    scaled[...] = ct[...].astype(F32) * on * gain_ref[...]

    def chip_total(i):
        return tot_row(2 * i) + tot_row(2 * i + 1)

    def f_join(i, state):
        f_copy(i, i).wait_recv()
        return jnp.exp(chip_total(i)) * state + f_in[pl.ds(i, 1)][0].astype(F32)

    state = lax.fori_loop(0, chip, f_join, state_ref[0])
    state = jnp.where(is_late, jnp.exp(tot_row(mate)) * state + other, state)
    start_state[...] = state.astype(BF16)

    for r in range(nb):
        sl = slice(r * T, (r + 1) * T)
        flat = att[sl, :] + rise_b[sl, :] * dot(q[sl, :], start_state[...], NN)
        att[sl, :] = flat
        stat[pl.ds(head, 1), r : r + 1, :] = jnp.sum(
            jnp.transpose(flat * flat), axis=0, keepdims=True
        )[None]
        stat[pl.ds(head, 1), nb + r : nb + r + 1, :] = jnp.sum(
            jnp.transpose(flat * scaled[sl, :]), axis=0, keepdims=True
        )[None]

    def h_copy(slot, to):
        return pltpu.make_async_remote_copy(
            src_ref=stat.at[head], dst_ref=stat.at[slot],
            send_sem=h_send.at[to], recv_sem=h_recv.at[slot],
            device_id={"head": to}, device_id_type=MESH,
        )

    def h_go(o, c):
        h_copy(head, lax.rem(head + o, m)).start()
        return c

    lax.fori_loop(1, m, h_go, 0)

    def h_join(o, acc):
        i = lax.rem(head + o, m)
        h_copy(i, i).wait_recv()
        return acc + stat[pl.ds(i, 1)][0]

    sums = lax.fori_loop(1, m, h_join, stat[pl.ds(head, 1)][0])
    inv = lax.rsqrt(sums[:nb] / width_all + 1e-06)
    coef = inv * inv * inv * sums[nb:] / width_all
    for r in range(nb):
        sl = slice(r * T, (r + 1) * T)
        inv_b = jnp.transpose(jnp.broadcast_to(inv[r : r + 1, :], (T, T)))
        coef_b = jnp.transpose(jnp.broadcast_to(coef[r : r + 1, :], (T, T)))
        flat = att[sl, :]
        grad[sl, :] = (inv_b * scaled[sl, :] - flat * coef_b).astype(BF16)
        att[sl, :] = flat * inv_b * gain_ref[...]

    back = dot(qr[...], grad[...], TN)
    swap_out[1] = back
    swap_copy(1).start()

    for r in range(nb):
        sl = slice(r * T, (r + 1) * T)
        on = jax.nn.sigmoid(gate[sl, :].astype(F32))
        normed = att[sl, :]
        out = (normed * on).astype(BF16)
        for part in range(T // piece):
            gated[r * (T // piece) + part] = out[part * piece : (part + 1) * piece]
        gg[sl, :] = (ct[sl, :].astype(F32) * normed * on * (1.0 - on)).astype(BF16)

    swap_copy(1).wait_recv()
    mine_b, other_b = swap_out[1], swap_in[1]
    earlier = jnp.exp(jnp.where(is_late, tot_row(mate), total))
    b_out[...] = (
        earlier * jnp.where(is_late, mine_b, other_b) + jnp.where(is_late, other_b, mine_b)
    ).astype(BF16)

    def b_copy(slot, to):
        return pltpu.make_async_remote_copy(
            src_ref=b_out, dst_ref=b_in.at[slot],
            send_sem=b_send.at[to], recv_sem=b_recv.at[slot],
            device_id={"ctx": 2 * to + core}, device_id_type=MESH,
        )

    def b_go(to, c):
        b_copy(chip, to).start()
        return c

    lax.fori_loop(0, chip, b_go, 0)

    def pick(d):
        def one(s, found):
            p = regroup[d * n + s]
            apart = lax.shift_right_logical(p, shift) - me
            return found + (1 - jnp.minimum(apart * apart, 1)) * (p & (n - 1))

        return lax.fori_loop(0, n, one, jnp.int32(0), unroll=8)

    def wanted(d):
        return gated[pick(d)]

    def a_copy(slot, to):
        return pltpu.make_async_remote_copy(
            src_ref=a_out.at[to], dst_ref=a_in.at[slot],
            send_sem=a_send.at[to], recv_sem=a_recv.at[slot],
            device_id={"ctx": to}, device_id_type=MESH,
        )

    def a_go(o, c):
        to = lax.rem(me + o, n)
        a_out[to] = wanted(to)
        a_copy(me, to).start()
        return c

    lax.fori_loop(1, n, a_go, 0)
    a_in[me] = wanted(me)

    for a in range(nb):
        w = (a + 1) * T
        sl = slice(a * T, w)
        ds = (dot(grad[sl, :], v[:w, :], NT) * mask[sl, :w]).astype(BF16)
        gq[sl, :] = (
            dot(ds, k[:w, :], NN) + rise_b[sl, :] * dot(grad[sl, :], start_state[...], NT)
        ).astype(BF16)
        dk = dot(ds, q[sl, :], TN)
        dv = dot(probs[sl, :w], grad[sl, :], TN)
        if a:
            gk_acc[: a * T, :] += dk[: a * T]
            gv_acc[: a * T, :] += dv[: a * T]
        gk_acc[sl, :] = dk[a * T :]
        gv_acc[sl, :] = dv[a * T :]

    def b_join(o, state):
        i = chips - 1 - o
        b_copy(i, i).wait_recv()
        return jnp.exp(chip_total(i)) * state + b_in[pl.ds(i, 1)][0].astype(F32)

    after = lax.fori_loop(0, chips - 1 - chip, b_join, jnp.zeros((T, T), F32))
    after = jnp.where(is_late, after, jnp.exp(tot_row(mate)) * after + other_b).astype(BF16)
    gk[...] = (gk_acc[...] + tail_b[...] * dot(v[...], after, NT)).astype(BF16)
    gv[...] = (gv_acc[...] + tail_b[...] * dot(k[...], after, NN)).astype(BF16)

    def a_wait(o, c):
        i = lax.rem(me + o, n)
        a_copy(i, i).wait_recv()
        return c

    lax.fori_loop(1, n, a_wait, 0)
    for s in range(n):
        src = lax.shift_right_logical(regroup[me * n + s], shift)
        go[s * piece : (s + 1) * piece, :] = a_in[src]

    swap_copy(0).wait_send()
    swap_copy(1).wait_send()

    def end_ctx(o, c):
        to = lax.rem(me + o, n)
        tot_copy(to, to).wait_send()
        a_copy(to, to).wait_send()
        return c

    lax.fori_loop(1, n, end_ctx, 0)

    def end_head(o, c):
        to = lax.rem(head + o, m)
        h_copy(to, to).wait_send()
        return c

    lax.fori_loop(1, m, end_head, 0)

    def end_f(to, c):
        f_copy(to, to).wait_send()
        return c

    lax.fori_loop(chip + 1, chips, end_f, 0)

    def end_b(to, c):
        b_copy(to, to).wait_send()
        return c

    lax.fori_loop(0, chip, end_b, 0)


def store(*refs):
    sem = refs[-1]
    copies = [
        pltpu.make_async_copy(refs[i], refs[5 + i], sem.at[i]) for i in range(5)
    ]
    for copy in copies:
        copy.start()
    for copy in copies:
        copy.wait()


def per_device(n, m, query, key, value, gate, decay, gain, state_in, cotangent, regroup):
    rows = query.shape[0]
    chips = n // 2
    nb = rows // T
    piece = rows // n
    big = lambda kind: pltpu.VMEM((rows, T), kind)
    dma = pltpu.SemaphoreType.DMA
    hbm = pl.BlockSpec(memory_space=pl.ANY)
    any_space = pl.BlockSpec(memory_space=pltpu.HBM)
    vmem = pl.BlockSpec(memory_space=pltpu.VMEM)
    results = pl.pallas_call(
        functools.partial(kernel, n, m, rows),
        out_shape=[jax.ShapeDtypeStruct((rows, T), BF16)] * 5,
        in_specs=[any_space] * 9,
        out_specs=[vmem] * 5,
        scratch_shapes=[big(BF16)] * 5
        + [
            pltpu.VMEM((nb, T), F32), pltpu.VMEM((1, T), F32), pltpu.VMEM((1, T, T), F32),
            pltpu.SMEM((n * n,), jnp.int32),
        ]
        + [big(F32)] * 3
        + [
            pltpu.VMEM((rows, rows), F32),
            pltpu.VMEM((rows, rows), BF16),
            big(F32), big(F32), pltpu.VMEM((n, piece, T), BF16), big(BF16), big(BF16), big(F32), big(F32),
        ]
        + [
            pltpu.VMEM((n, 8, T), F32),
            pltpu.VMEM((2, T, T), F32),
            pltpu.VMEM((2, T, T), F32),
            pltpu.VMEM((T, T), BF16),
            pltpu.VMEM((chips, T, T), BF16),
            pltpu.VMEM((T, T), BF16),
            pltpu.VMEM((chips, T, T), BF16),
            pltpu.VMEM((m, 2 * nb, T), F32),
            pltpu.VMEM((n, piece, T), BF16),
            pltpu.VMEM((n, piece, T), BF16),
            pltpu.VMEM((T, T), BF16),
        ]
        + [
            dma((9,)), dma((n,)), dma((n,)), dma((2,)), dma((2,)),
            dma((chips,)), dma((chips,)), dma((chips,)), dma((chips,)),
            dma((m,)), dma((m,)), dma((n,)), dma((n,)),
        ],
        compiler_params=pltpu.CompilerParams(
            collective_id=0, has_side_effects=True, vmem_limit_bytes=40 << 20
        ),
        name="layer",
    )(
        *[
            pltpu.with_memory_space_constraint(x, pltpu.HBM)
            for x in (
                query, key, value, gate, cotangent,
                decay.reshape((nb, T)), gain.reshape((1, T)), state_in, regroup,
            )
        ]
    )
    return pl.pallas_call(
        store,
        out_shape=[jax.ShapeDtypeStruct((rows, T), BF16)] * 5,
        in_specs=[hbm] * 5,
        out_specs=[any_space] * 5,
        scratch_shapes=[dma((5,))],
        compiler_params=pltpu.CompilerParams(vmem_limit_bytes=1 << 20),
        name="store",
    )(*results)


def solution(mesh):
    rows = P("ctx", "head")
    in_specs = (rows, rows, rows, rows, rows, P("head"), P("head", None, None), rows, P())
    body = functools.partial(per_device, mesh.shape["ctx"], mesh.shape["head"])
    return jax.shard_map(
        body, mesh=mesh, in_specs=in_specs, out_specs=(rows,) * 5, check_vma=False
    )
```

```python
import functools

import jax
import jax.numpy as jnp
from jax import lax
from jax.experimental import pallas as pl
from jax.experimental.pallas import tpu as pltpu
from jax.sharding import PartitionSpec as P

F32 = jnp.float32
BF16 = jnp.bfloat16
MESH = pl.DeviceIdType.MESH
T = 128
NT = (((1,), (1,)), ((), ()))
NN = (((1,), (0,)), ((), ()))
TN = (((0,), (0,)), ((), ()))


def dot(a, b, dims):
    return lax.dot_general(a, b, dims, preferred_element_type=F32)


def columns(rows):
    filler = jnp.zeros((T - sum(x.shape[0] for x in rows), T), F32)
    return jnp.transpose(jnp.concatenate([*rows, filler], axis=0))


def row_sums(x):
    high = x.astype(BF16)
    low = (x - high.astype(F32)).astype(BF16)
    ones = jnp.ones((8, T), BF16)
    return dot(ones, high, NT) + dot(ones, low, NT)


def kernel(
    n, m, rows,
    q_hbm, k_hbm, v_hbm, gate_hbm, ct_hbm, decay_hbm, gain_hbm, state_hbm, regroup_hbm,
    go, gq, gk, gv, gg,
    q, k, v, gate, ct, decay_ref, gain_ref, state_ref, regroup,
    cum_b, rise_b, tail_b, mask, probs, att, scaled, gated, grad, qr, gk_acc, gv_acc,
    tots, swap_out, swap_in, f_out, f_in, b_out, b_in, stat, a_out, a_in, start_state, inv_rows, inv_part, picks,
    in_sem, tot_send, tot_recv, swap_send, swap_recv,
    f_send, f_recv, b_send, b_recv, h_send, h_recv, a_send, a_recv, i_send, i_recv,
):
    me = lax.axis_index("ctx")
    head = lax.axis_index("head")
    chip = me // 2
    core = me % 2
    mate = me + 1 - 2 * core
    chips = n // 2
    nb = rows // T
    piece = rows // n
    width_all = m * T
    shift = n.bit_length() - 1

    loads = [
        pltpu.make_async_copy(src, dst, in_sem.at[i])
        for i, (src, dst) in enumerate(
            [
                (k_hbm, k), (v_hbm, v), (q_hbm, q), (gate_hbm, gate), (ct_hbm, ct),
                (decay_hbm, decay_ref), (gain_hbm, gain_ref), (state_hbm, state_ref),
                (regroup_hbm, regroup),
            ]
        )
    ]
    for i in (5, 0, 1, 2, 3, 4, 6, 7, 8):
        loads[i].start()

    barrier = pltpu.get_barrier_semaphore()

    def greet_ctx(o, c):
        pl.semaphore_signal(
            barrier, inc=1, device_id={"ctx": lax.rem(me + o, n)}, device_id_type=MESH
        )
        return c

    def greet_head(o, c):
        pl.semaphore_signal(
            barrier, inc=1, device_id={"head": lax.rem(head + o, m)}, device_id_type=MESH
        )
        return c

    lax.fori_loop(1, n, greet_ctx, 0)
    lax.fori_loop(1, m, greet_head, 0)

    row_i = lax.broadcasted_iota(jnp.int32, (T, T), 0)
    col_i = lax.broadcasted_iota(jnp.int32, (T, T), 1)
    upper = (row_i <= col_i).astype(F32)
    loads[5].wait()
    partial_sums = lax.dot_general(
        decay_ref[...], upper, NN, precision=lax.Precision.HIGHEST, preferred_element_type=F32
    )
    crow = []
    offset = jnp.zeros((1, 1), F32)
    for r in range(nb):
        row = partial_sums[r : r + 1, :]
        crow.append(row + offset)
        offset = offset + row[:, T - 1 : T]
    total = jnp.broadcast_to(crow[-1][:, T - 1 : T], (1, T))
    tots[pl.ds(me, 1)] = jnp.broadcast_to(total, (8, T))[None]
    cols = columns(crow)
    for r in range(nb):
        sl = slice(r * T, (r + 1) * T)
        cb = jnp.broadcast_to(cols[:, r : r + 1], (T, T))
        cum_b[sl, :] = cb
        rise_b[sl, :] = jnp.exp(cb)
        tail_b[sl, :] = jnp.exp(total - cb)

    loads[0].wait()
    loads[1].wait()
    weighted = (k[...].astype(F32) * tail_b[...]).astype(BF16)
    local = dot(weighted, v[...], TN)
    swap_out[0] = local

    pl.semaphore_wait(barrier, n - 1 + m - 1)

    def swap_copy(i):
        return pltpu.make_async_remote_copy(
            src_ref=swap_out.at[i], dst_ref=swap_in.at[i],
            send_sem=swap_send.at[i], recv_sem=swap_recv.at[i],
            device_id={"ctx": mate}, device_id_type=MESH,
        )

    swap_copy(0).start()

    def tot_copy(slot, to):
        return pltpu.make_async_remote_copy(
            src_ref=tots.at[me], dst_ref=tots.at[slot],
            send_sem=tot_send.at[to], recv_sem=tot_recv.at[slot],
            device_id={"ctx": to}, device_id_type=MESH,
        )

    def tot_go(o, c):
        tot_copy(me, lax.rem(me + o, n)).start()
        return c

    lax.fori_loop(1, n, tot_go, 0)

    loads[2].wait()
    causal = row_i >= col_i

    def decay_tile(a, b):
        diff = cum_b[a * T : (a + 1) * T, :] - crow[b]
        if a == b:
            return jnp.where(causal, jnp.exp(jnp.where(causal, diff, 0.0)), 0.0)
        return jnp.exp(diff)

    def scores_for(a):
        w = (a + 1) * T
        s = dot(q[a * T : w, :], k[:w, :], NT)
        for b in range(a + 1):
            d = decay_tile(a, b)
            mask[a * T : w, b * T : (b + 1) * T] = d
            probs[a * T : w, b * T : (b + 1) * T] = (s[:, b * T : (b + 1) * T] * d).astype(BF16)

    half = nb // 4
    for a in range(half):
        scores_for(a)

    def tot_wait(o, c):
        i = lax.rem(2 * chip + o, n)
        tot_copy(i, i).wait_recv()
        return c

    swap_copy(0).wait_recv()
    tot_copy(mate, mate).wait_recv()

    def tot_row(i):
        return tots[pl.ds(i, 1)][0, 0:1, :]

    mine, other = swap_out[0], swap_in[0]
    is_late = core == 1
    later = jnp.exp(jnp.where(is_late, total, tot_row(mate)))
    f_out[...] = (later * jnp.where(is_late, other, mine) + jnp.where(is_late, mine, other)).astype(BF16)

    def f_copy(slot, to):
        return pltpu.make_async_remote_copy(
            src_ref=f_out, dst_ref=f_in.at[slot],
            send_sem=f_send.at[to], recv_sem=f_recv.at[slot],
            device_id={"ctx": 2 * to + core}, device_id_type=MESH,
        )

    def f_go(to, c):
        f_copy(chip, to).start()
        return c

    lax.fori_loop(chip + 1, chips, f_go, 0)

    for a in range(half, nb):
        scores_for(a)
    for a in range(nb):
        w = (a + 1) * T
        att[a * T : w, :] = dot(probs[a * T : w, :w], v[:w, :], NN)
    qr[...] = jnp.transpose((q[...].astype(F32) * rise_b[...]).astype(BF16))
    loads[3].wait()
    for i in (4, 6, 7, 8):
        loads[i].wait()
    on = jax.nn.sigmoid(gate[...].astype(F32))
    scaled[...] = ct[...].astype(F32) * on * gain_ref[...]

    def pick(d):
        def one(s, found):
            p = regroup[d * n + s]
            apart = lax.shift_right_logical(p, shift) - me
            return found + (1 - jnp.minimum(apart * apart, 1)) * (p & (n - 1))

        return lax.fori_loop(0, n, one, jnp.int32(0), unroll=8)

    def pick_store(d, c):
        picks[d] = pick(d)
        return c

    lax.fori_loop(0, n, pick_store, 0)

    def chip_total(i):
        return tot_row(2 * i) + tot_row(2 * i + 1)

    def f_join(i, state):
        f_copy(i, i).wait_recv()
        return jnp.exp(chip_total(i)) * state + f_in[pl.ds(i, 1)][0].astype(F32)

    lax.fori_loop(2, n, tot_wait, 0)
    state = lax.fori_loop(0, chip, f_join, state_ref[0])
    state = jnp.where(is_late, jnp.exp(tot_row(mate)) * state + other, state)
    start_state[...] = state.astype(BF16)

    for r in range(nb):
        sl = slice(r * T, (r + 1) * T)
        flat = att[sl, :] + rise_b[sl, :] * dot(q[sl, :], start_state[...], NN)
        att[sl, :] = flat
        squares = row_sums(flat * flat)[0:1]
        cross = row_sums(flat * scaled[sl, :])[0:1]
        stat[pl.ds(head, 1), r : r + 1, :] = squares[None]
        stat[pl.ds(head, 1), nb + r : nb + r + 1, :] = cross[None]

    def h_copy(slot, to):
        return pltpu.make_async_remote_copy(
            src_ref=stat.at[head], dst_ref=stat.at[slot],
            send_sem=h_send.at[to], recv_sem=h_recv.at[slot],
            device_id={"head": to}, device_id_type=MESH,
        )

    def h_go(o, c):
        h_copy(head, lax.rem(head + o, m)).start()
        return c

    lax.fori_loop(1, m, h_go, 0)

    per_tile = T // piece
    for r in range(nb):
        sl = slice(r * T, (r + 1) * T)
        on = jax.nn.sigmoid(gate[sl, :].astype(F32))
        out = (att[sl, :] * gain_ref[...] * on).astype(BF16)
        for part in range(per_tile):
            gated[r * per_tile + part] = out[part * piece : (part + 1) * piece]

    def wanted(d):
        return gated[picks[d]]

    def a_copy(slot, to):
        return pltpu.make_async_remote_copy(
            src_ref=a_out.at[to], dst_ref=a_in.at[slot],
            send_sem=a_send.at[to], recv_sem=a_recv.at[slot],
            device_id={"ctx": to}, device_id_type=MESH,
        )

    def a_go(o, c):
        to = lax.rem(me + o, n)
        a_out[to] = wanted(to)
        a_copy(me, to).start()
        return c

    lax.fori_loop(1, n, a_go, 0)
    a_in[me] = wanted(me)

    def h_join(o, acc):
        i = lax.rem(head + o, m)
        h_copy(i, i).wait_recv()
        return acc + stat[pl.ds(i, 1)][0]

    sums = lax.fori_loop(1, m, h_join, stat[pl.ds(head, 1)][0])
    inv = lax.rsqrt(sums[:nb] / width_all + 1e-06)
    coef = inv * inv * inv * sums[nb:] / width_all
    inv_rows[pl.ds(me, 1)] = inv[None]
    cols = columns([inv, coef])
    for r in range(nb):
        sl = slice(r * T, (r + 1) * T)
        inv_b = jnp.broadcast_to(cols[:, r : r + 1], (T, T))
        coef_b = jnp.broadcast_to(cols[:, nb + r : nb + r + 1], (T, T))
        flat = att[sl, :]
        grad[sl, :] = (inv_b * scaled[sl, :] - flat * coef_b).astype(BF16)
        att[sl, :] = flat * inv_b

    back = dot(qr[...], grad[...], NN)
    swap_out[1] = back
    swap_copy(1).start()

    def i_copy(slot, to):
        return pltpu.make_async_remote_copy(
            src_ref=inv_rows.at[me], dst_ref=inv_rows.at[slot],
            send_sem=i_send.at[to], recv_sem=i_recv.at[slot],
            device_id={"ctx": to}, device_id_type=MESH,
        )

    def i_go(o, c):
        to = lax.rem(me + o, n)
        i_copy(me, to).start()
        return c

    lax.fori_loop(1, n, i_go, 0)

    for r in range(nb):
        sl = slice(r * T, (r + 1) * T)
        on = jax.nn.sigmoid(gate[sl, :].astype(F32))
        normed = att[sl, :] * gain_ref[...]
        gg[sl, :] = (ct[sl, :].astype(F32) * normed * on * (1.0 - on)).astype(BF16)

    swap_copy(1).wait_recv()
    mine_b, other_b = swap_out[1], swap_in[1]
    earlier = jnp.exp(jnp.where(is_late, tot_row(mate), total))
    b_out[...] = (
        earlier * jnp.where(is_late, mine_b, other_b) + jnp.where(is_late, other_b, mine_b)
    ).astype(BF16)

    def b_copy(slot, to):
        return pltpu.make_async_remote_copy(
            src_ref=b_out, dst_ref=b_in.at[slot],
            send_sem=b_send.at[to], recv_sem=b_recv.at[slot],
            device_id={"ctx": 2 * to + core}, device_id_type=MESH,
        )

    def b_go(to, c):
        b_copy(chip, to).start()
        return c

    lax.fori_loop(0, chip, b_go, 0)

    for a in range(nb):
        w = (a + 1) * T
        sl = slice(a * T, w)
        ds = (dot(grad[sl, :], v[:w, :], NT) * mask[sl, :w]).astype(BF16)
        gq[sl, :] = (
            dot(ds, k[:w, :], NN) + rise_b[sl, :] * dot(grad[sl, :], start_state[...], NT)
        ).astype(BF16)
        dk = dot(ds, q[sl, :], TN)
        dv = dot(probs[sl, :w], grad[sl, :], TN)
        if a:
            gk_acc[: a * T, :] += dk[: a * T]
            gv_acc[: a * T, :] += dv[: a * T]
        gk_acc[sl, :] = dk[a * T :]
        gv_acc[sl, :] = dv[a * T :]

    def a_wait(o, c):
        i = lax.rem(me + o, n)
        a_copy(i, i).wait_recv()
        i_copy(i, i).wait_recv()
        return c

    lax.fori_loop(1, n, a_wait, 0)
    lane_row = lax.broadcasted_iota(jnp.int32, (nb, T), 0)
    chosen = []
    for s in range(n):
        p = regroup[me * n + s]
        apart = lane_row - lax.shift_right_logical(p & (n - 1), per_tile.bit_length() - 1)
        here = (1 - jnp.minimum(apart * apart, 1)).astype(F32)
        tile = inv_rows[lax.shift_right_logical(p, shift)]
        chosen.append(jnp.sum(tile * here, axis=0, keepdims=True))
    cols = columns(chosen)
    for s in range(n):
        p = regroup[me * n + s]
        inv_b = jnp.broadcast_to(cols[:, s : s + 1], (T, T))
        if per_tile > 1:
            for part in range(per_tile):
                inv_part[part] = inv_b[part * piece : (part + 1) * piece]
            inv_b = inv_part[p & (per_tile - 1)]
        arrived = a_in[lax.shift_right_logical(p, shift)].astype(F32)
        go[s * piece : (s + 1) * piece, :] = (arrived * inv_b).astype(BF16)

    def b_join(o, state):
        i = chips - 1 - o
        b_copy(i, i).wait_recv()
        return jnp.exp(chip_total(i)) * state + b_in[pl.ds(i, 1)][0].astype(F32)

    after = lax.fori_loop(0, chips - 1 - chip, b_join, jnp.zeros((T, T), F32))
    after = jnp.where(is_late, after, jnp.exp(tot_row(mate)) * after + other_b).astype(BF16)
    gk[...] = (gk_acc[...] + tail_b[...] * dot(v[...], after, NT)).astype(BF16)
    gv[...] = (gv_acc[...] + tail_b[...] * dot(k[...], after, NN)).astype(BF16)

    swap_copy(0).wait_send()
    swap_copy(1).wait_send()

    def end_ctx(o, c):
        to = lax.rem(me + o, n)
        tot_copy(to, to).wait_send()
        a_copy(to, to).wait_send()
        i_copy(to, to).wait_send()
        return c

    lax.fori_loop(1, n, end_ctx, 0)

    def end_head(o, c):
        to = lax.rem(head + o, m)
        h_copy(to, to).wait_send()
        return c

    lax.fori_loop(1, m, end_head, 0)

    def end_f(to, c):
        f_copy(to, to).wait_send()
        return c

    lax.fori_loop(chip + 1, chips, end_f, 0)

    def end_b(to, c):
        b_copy(to, to).wait_send()
        return c

    lax.fori_loop(0, chip, end_b, 0)


def store(*refs):
    sem = refs[-1]
    copies = [
        pltpu.make_async_copy(refs[i], refs[5 + i], sem.at[i]) for i in range(5)
    ]
    for copy in copies:
        copy.start()
    for copy in copies:
        copy.wait()


def per_device(n, m, query, key, value, gate, decay, gain, state_in, cotangent, regroup):
    rows = query.shape[0]
    chips = n // 2
    nb = rows // T
    piece = rows // n
    big = lambda kind: pltpu.VMEM((rows, T), kind)
    dma = pltpu.SemaphoreType.DMA
    hbm = pl.BlockSpec(memory_space=pl.ANY)
    any_space = pl.BlockSpec(memory_space=pltpu.HBM)
    vmem = pl.BlockSpec(memory_space=pltpu.VMEM)
    results = pl.pallas_call(
        functools.partial(kernel, n, m, rows),
        out_shape=[jax.ShapeDtypeStruct((rows, T), BF16)] * 5,
        in_specs=[any_space] * 9,
        out_specs=[vmem] * 5,
        scratch_shapes=[big(BF16)] * 5
        + [
            pltpu.VMEM((nb, T), F32), pltpu.VMEM((1, T), F32), pltpu.VMEM((1, T, T), F32),
            pltpu.SMEM((n * n,), jnp.int32),
        ]
        + [big(F32)] * 3
        + [
            pltpu.VMEM((rows, rows), F32),
            pltpu.VMEM((rows, rows), BF16),
            big(F32), big(F32), pltpu.VMEM((n, piece, T), BF16), big(BF16), pltpu.VMEM((T, rows), BF16), big(F32), big(F32),
        ]
        + [
            pltpu.VMEM((n, 8, T), F32),
            pltpu.VMEM((2, T, T), F32),
            pltpu.VMEM((2, T, T), F32),
            pltpu.VMEM((T, T), BF16),
            pltpu.VMEM((chips, T, T), BF16),
            pltpu.VMEM((T, T), BF16),
            pltpu.VMEM((chips, T, T), BF16),
            pltpu.VMEM((m, 2 * nb, T), F32),
            pltpu.VMEM((n, piece, T), BF16),
            pltpu.VMEM((n, piece, T), BF16),
            pltpu.VMEM((T, T), BF16),
            pltpu.VMEM((n, nb, T), F32),
            pltpu.VMEM((T // piece, piece, T), F32),
            pltpu.SMEM((n,), jnp.int32),
        ]
        + [
            dma((9,)), dma((n,)), dma((n,)), dma((2,)), dma((2,)),
            dma((chips,)), dma((chips,)), dma((chips,)), dma((chips,)),
            dma((m,)), dma((m,)), dma((n,)), dma((n,)), dma((n,)), dma((n,)),
        ],
        compiler_params=pltpu.CompilerParams(
            collective_id=0, has_side_effects=True, vmem_limit_bytes=40 << 20
        ),
        name="layer",
    )(
        *[
            pltpu.with_memory_space_constraint(x, pltpu.HBM)
            for x in (
                query, key, value, gate, cotangent,
                decay.reshape((nb, T)), gain.reshape((1, T)), state_in, regroup,
            )
        ]
    )
    return pl.pallas_call(
        store,
        out_shape=[jax.ShapeDtypeStruct((rows, T), BF16)] * 5,
        in_specs=[hbm] * 5,
        out_specs=[any_space] * 5,
        scratch_shapes=[dma((5,))],
        compiler_params=pltpu.CompilerParams(vmem_limit_bytes=1 << 20),
        name="store",
    )(*results)


def solution(mesh):
    rows = P("ctx", "head")
    in_specs = (rows, rows, rows, rows, rows, P("head"), P("head", None, None), rows, P())
    body = functools.partial(per_device, mesh.shape["ctx"], mesh.shape["head"])
    return jax.shard_map(
        body, mesh=mesh, in_specs=in_specs, out_specs=(rows,) * 5, check_vma=False
    )
```

```python
import functools

import jax
import jax.numpy as jnp
from jax import lax
from jax.experimental import pallas as pl
from jax.experimental.pallas import tpu as pltpu
from jax.sharding import PartitionSpec as P

F32 = jnp.float32
BF16 = jnp.bfloat16
MESH = pl.DeviceIdType.MESH
T = 128
NT = (((1,), (1,)), ((), ()))
NN = (((1,), (0,)), ((), ()))
TN = (((0,), (0,)), ((), ()))


def dot(a, b, dims):
    return lax.dot_general(a, b, dims, preferred_element_type=F32)


def columns(rows):
    filler = jnp.zeros((T - sum(x.shape[0] for x in rows), T), F32)
    return jnp.transpose(jnp.concatenate([*rows, filler], axis=0))


def row_sums(x):
    high = x.astype(BF16)
    low = (x - high.astype(F32)).astype(BF16)
    ones = jnp.ones((8, T), BF16)
    return dot(ones, high, NT) + dot(ones, low, NT)


def kernel(
    n, m, rows,
    q_hbm, k_hbm, v_hbm, gate_hbm, ct_hbm, decay_hbm, gain_hbm, state_hbm, regroup_hbm,
    go, gq, gk, gv, gg,
    q, k, v, gate, ct, decay_ref, gain_ref, state_ref, regroup,
    cum_b, rise_b, tail_b, mask, probs, att, scaled, on_b, gated, grad, qr, gk_acc, gv_acc,
    tots, swap_out, swap_in, f_out, f_in, b_out, b_in, stat, a_out, a_in, start_state, inv_rows, inv_part, picks, ds, probs_t,
    in_sem, tot_send, tot_recv, swap_send, swap_recv,
    f_send, f_recv, b_send, b_recv, h_send, h_recv, a_send, a_recv, i_send, i_recv,
):
    me = lax.axis_index("ctx")
    head = lax.axis_index("head")
    chip = me // 2
    core = me % 2
    mate = me + 1 - 2 * core
    chips = n // 2
    nb = rows // T
    piece = rows // n
    width_all = m * T
    per_block = 2
    G = per_block * T
    groups = rows // G
    shift = n.bit_length() - 1

    loads = [
        pltpu.make_async_copy(src, dst, in_sem.at[i])
        for i, (src, dst) in enumerate(
            [
                (k_hbm, k), (v_hbm, v), (q_hbm, q), (gate_hbm, gate), (ct_hbm, ct),
                (decay_hbm, decay_ref), (gain_hbm, gain_ref), (state_hbm, state_ref),
                (regroup_hbm, regroup),
            ]
        )
    ]
    for i in (5, 0, 1, 2, 3, 4, 6, 7, 8):
        loads[i].start()

    barrier = pltpu.get_barrier_semaphore()

    def greet_ctx(o, c):
        pl.semaphore_signal(
            barrier, inc=1, device_id={"ctx": lax.rem(me + o, n)}, device_id_type=MESH
        )
        return c

    def greet_head(o, c):
        pl.semaphore_signal(
            barrier, inc=1, device_id={"head": lax.rem(head + o, m)}, device_id_type=MESH
        )
        return c

    lax.fori_loop(1, n, greet_ctx, 0)
    lax.fori_loop(1, m, greet_head, 0)

    row_i = lax.broadcasted_iota(jnp.int32, (T, T), 0)
    col_i = lax.broadcasted_iota(jnp.int32, (T, T), 1)
    upper = (row_i <= col_i).astype(F32)
    loads[5].wait()
    partial_sums = lax.dot_general(
        decay_ref[...], upper, NN, precision=lax.Precision.HIGHEST, preferred_element_type=F32
    )
    crow = []
    offset = jnp.zeros((1, 1), F32)
    for r in range(nb):
        row = partial_sums[r : r + 1, :]
        crow.append(row + offset)
        offset = offset + row[:, T - 1 : T]
    total = jnp.broadcast_to(crow[-1][:, T - 1 : T], (1, T))
    tots[pl.ds(me, 1)] = total[None]
    cols = columns(crow)
    for r in range(nb):
        sl = slice(r * T, (r + 1) * T)
        cb = jnp.broadcast_to(cols[:, r : r + 1], (T, T))
        cum_b[sl, :] = cb
        rise_b[sl, :] = jnp.exp(cb)
        tail_b[sl, :] = jnp.exp(total - cb)

    loads[0].wait()
    loads[1].wait()
    weighted = (k[...].astype(F32) * tail_b[...]).astype(BF16)
    local = dot(weighted, v[...], TN)
    swap_out[0] = local

    pl.semaphore_wait(barrier, n - 1 + m - 1)

    def swap_copy(i):
        return pltpu.make_async_remote_copy(
            src_ref=swap_out.at[i], dst_ref=swap_in.at[i],
            send_sem=swap_send.at[i], recv_sem=swap_recv.at[i],
            device_id={"ctx": mate}, device_id_type=MESH,
        )

    swap_copy(0).start()

    def tot_copy(slot, to):
        return pltpu.make_async_remote_copy(
            src_ref=tots.at[me], dst_ref=tots.at[slot],
            send_sem=tot_send.at[to], recv_sem=tot_recv.at[slot],
            device_id={"ctx": to}, device_id_type=MESH,
        )

    def tot_go(o, c):
        tot_copy(me, lax.rem(me + o, n)).start()
        return c

    lax.fori_loop(1, n, tot_go, 0)

    loads[2].wait()
    causal = row_i >= col_i

    def decay_tile(a, b):
        diff = cum_b[a * T : (a + 1) * T, :] - crow[b]
        if a < b:
            return jnp.zeros((T, T), F32)
        if a == b:
            return jnp.where(causal, jnp.exp(jnp.where(causal, diff, 0.0)), 0.0)
        return jnp.exp(diff)

    def scores_for(g):
        w = (g + 1) * G
        s = dot(q[g * G : w, :], k[:w, :], NT)
        for a in range(g * per_block, (g + 1) * per_block):
            up = a * T - g * G
            for b in range(w // T):
                at = (slice(a * T, (a + 1) * T), slice(b * T, (b + 1) * T))
                d = decay_tile(a, b)
                mask[at] = d
                probs[at] = (s[up : up + T, b * T : (b + 1) * T] * d).astype(BF16)

    half = groups // 2
    for a in range(half):
        scores_for(a)

    def tot_wait(o, c):
        i = lax.rem(2 * chip + o, n)
        tot_copy(i, i).wait_recv()
        return c

    swap_copy(0).wait_recv()
    tot_copy(mate, mate).wait_recv()

    def tot_row(i):
        return tots[pl.ds(i, 1)][0]

    mine, other = swap_out[0], swap_in[0]
    is_late = core == 1
    later = jnp.exp(jnp.where(is_late, total, tot_row(mate)))
    f_out[...] = (later * jnp.where(is_late, other, mine) + jnp.where(is_late, mine, other)).astype(BF16)

    def f_copy(slot, to):
        return pltpu.make_async_remote_copy(
            src_ref=f_out, dst_ref=f_in.at[slot],
            send_sem=f_send.at[to], recv_sem=f_recv.at[slot],
            device_id={"ctx": 2 * to + core}, device_id_type=MESH,
        )

    def f_go(to, c):
        f_copy(chip, to).start()
        return c

    lax.fori_loop(chip + 1, chips, f_go, 0)

    for a in range(half, groups):
        scores_for(a)
    for g in range(groups):
        w = (g + 1) * G
        att[g * G : w, :] = dot(probs[g * G : w, :w], v[:w, :], NN)
    loads[3].wait()
    for i in (4, 6, 7, 8):
        loads[i].wait()
    on_b[...] = jax.nn.sigmoid(gate[...].astype(F32))
    scaled[...] = ct[...].astype(F32) * on_b[...] * gain_ref[...]

    def pick(d):
        def one(s, found):
            p = regroup[d * n + s]
            apart = lax.shift_right_logical(p, shift) - me
            return found + (1 - jnp.minimum(apart * apart, 1)) * (p & (n - 1))

        return lax.fori_loop(0, n, one, jnp.int32(0), unroll=8)

    def pick_store(d, c):
        picks[d] = pick(d)
        return c

    def chip_total(i):
        return tot_row(2 * i) + tot_row(2 * i + 1)

    def f_join(i, state):
        f_copy(i, i).wait_recv()
        return jnp.exp(chip_total(i)) * state + f_in[pl.ds(i, 1)][0].astype(F32)

    lax.fori_loop(2, n, tot_wait, 0)
    state = lax.fori_loop(0, chip, f_join, state_ref[0])
    state = jnp.where(is_late, jnp.exp(tot_row(mate)) * state + other, state)
    start_state[...] = state.astype(BF16)

    for r in range(nb):
        sl = slice(r * T, (r + 1) * T)
        flat = att[sl, :] + rise_b[sl, :] * dot(q[sl, :], start_state[...], NN)
        att[sl, :] = flat
        squares = row_sums(flat * flat)[0:1]
        cross = row_sums(flat * scaled[sl, :])[0:1]
        stat[pl.ds(head, 1), r : r + 1, :] = squares[None]
        stat[pl.ds(head, 1), nb + r : nb + r + 1, :] = cross[None]

    def h_copy(slot, to):
        return pltpu.make_async_remote_copy(
            src_ref=stat.at[head], dst_ref=stat.at[slot],
            send_sem=h_send.at[to], recv_sem=h_recv.at[slot],
            device_id={"head": to}, device_id_type=MESH,
        )

    def h_go(o, c):
        h_copy(head, lax.rem(head + o, m)).start()
        return c

    lax.fori_loop(1, m, h_go, 0)

    lax.fori_loop(0, n, pick_store, 0)
    per_tile = T // piece
    for r in range(nb):
        sl = slice(r * T, (r + 1) * T)
        on = on_b[sl, :]
        out = (att[sl, :] * gain_ref[...] * on).astype(BF16)
        for part in range(per_tile):
            gated[r * per_tile + part] = out[part * piece : (part + 1) * piece]

    def wanted(d):
        return gated[picks[d]]

    def a_copy(slot, to):
        return pltpu.make_async_remote_copy(
            src_ref=a_out.at[to], dst_ref=a_in.at[slot],
            send_sem=a_send.at[to], recv_sem=a_recv.at[slot],
            device_id={"ctx": to}, device_id_type=MESH,
        )

    def a_go(o, c):
        to = lax.rem(me + o, n)
        a_out[to] = wanted(to)
        a_copy(me, to).start()
        return c

    lax.fori_loop(1, n, a_go, 0)
    a_in[me] = wanted(me)

    qr[...] = jnp.transpose((q[...].astype(F32) * rise_b[...]).astype(BF16))
    for g in range(groups):
        sl = slice(g * G, (g + 1) * G)
        probs_t[sl, g * G :] = jnp.transpose(probs[g * G :, sl])

    def h_join(o, acc):
        i = lax.rem(head + o, m)
        h_copy(i, i).wait_recv()
        return acc + stat[pl.ds(i, 1)][0]

    sums = lax.fori_loop(1, m, h_join, stat[pl.ds(head, 1)][0])
    inv = lax.rsqrt(sums[:nb] / width_all + 1e-06)
    coef = inv * inv * inv * sums[nb:] / width_all
    inv_rows[pl.ds(me, 1)] = inv[None]
    cols = columns([inv, coef])
    for r in range(nb):
        sl = slice(r * T, (r + 1) * T)
        inv_b = jnp.broadcast_to(cols[:, r : r + 1], (T, T))
        coef_b = jnp.broadcast_to(cols[:, nb + r : nb + r + 1], (T, T))
        flat = att[sl, :]
        grad[sl, :] = (inv_b * scaled[sl, :] - flat * coef_b).astype(BF16)
        att[sl, :] = flat * inv_b

    back = dot(qr[...], grad[...], NN)
    swap_out[1] = back
    swap_copy(1).start()

    def i_copy(slot, to):
        return pltpu.make_async_remote_copy(
            src_ref=inv_rows.at[me], dst_ref=inv_rows.at[slot],
            send_sem=i_send.at[to], recv_sem=i_recv.at[slot],
            device_id={"ctx": to}, device_id_type=MESH,
        )

    def i_go(o, c):
        to = lax.rem(me + o, n)
        i_copy(me, to).start()
        return c

    lax.fori_loop(1, n, i_go, 0)

    for r in range(nb):
        sl = slice(r * T, (r + 1) * T)
        on = on_b[sl, :]
        normed = att[sl, :] * gain_ref[...]
        gg[sl, :] = (ct[sl, :].astype(F32) * normed * on * (1.0 - on)).astype(BF16)

    swap_copy(1).wait_recv()
    mine_b, other_b = swap_out[1], swap_in[1]
    earlier = jnp.exp(jnp.where(is_late, tot_row(mate), total))
    b_out[...] = (
        earlier * jnp.where(is_late, mine_b, other_b) + jnp.where(is_late, other_b, mine_b)
    ).astype(BF16)

    def b_copy(slot, to):
        return pltpu.make_async_remote_copy(
            src_ref=b_out, dst_ref=b_in.at[slot],
            send_sem=b_send.at[to], recv_sem=b_recv.at[slot],
            device_id={"ctx": 2 * to + core}, device_id_type=MESH,
        )

    def b_go(to, c):
        b_copy(chip, to).start()
        return c

    lax.fori_loop(0, chip, b_go, 0)

    for g in range(groups):
        w = (g + 1) * G
        sl = slice(g * G, w)
        ds[sl, :w] = (dot(grad[sl, :], v[:w, :], NT) * mask[sl, :w]).astype(BF16)
        gq[sl, :] = (
            dot(ds[sl, :w], k[:w, :], NN)
            + rise_b[sl, :] * dot(grad[sl, :], start_state[...], NT)
        ).astype(BF16)
    for g in range(groups):
        sl = slice(g * G, (g + 1) * G)
        gk_acc[sl, :] = dot(ds[g * G :, sl], q[g * G :, :], TN)
        gv_acc[sl, :] = dot(probs_t[sl, g * G :], grad[g * G :, :], NN)

    def a_wait(o, c):
        i = lax.rem(me + o, n)
        a_copy(i, i).wait_recv()
        i_copy(i, i).wait_recv()
        return c

    lax.fori_loop(1, n, a_wait, 0)
    lane_row = lax.broadcasted_iota(jnp.int32, (nb, T), 0)
    chosen = []
    for s in range(n):
        p = regroup[me * n + s]
        apart = lane_row - lax.shift_right_logical(p & (n - 1), per_tile.bit_length() - 1)
        here = (1 - jnp.minimum(apart * apart, 1)).astype(F32)
        tile = inv_rows[lax.shift_right_logical(p, shift)]
        chosen.append(jnp.sum(tile * here, axis=0, keepdims=True))
    cols = columns(chosen)
    for s in range(n):
        p = regroup[me * n + s]
        inv_b = jnp.broadcast_to(cols[:, s : s + 1], (T, T))
        if per_tile > 1:
            for part in range(per_tile):
                inv_part[part] = inv_b[part * piece : (part + 1) * piece]
            inv_b = inv_part[p & (per_tile - 1)]
        arrived = a_in[lax.shift_right_logical(p, shift)].astype(F32)
        go[s * piece : (s + 1) * piece, :] = (arrived * inv_b).astype(BF16)

    def b_join(o, state):
        i = chips - 1 - o
        b_copy(i, i).wait_recv()
        return jnp.exp(chip_total(i)) * state + b_in[pl.ds(i, 1)][0].astype(F32)

    after = lax.fori_loop(0, chips - 1 - chip, b_join, jnp.zeros((T, T), F32))
    after = jnp.where(is_late, after, jnp.exp(tot_row(mate)) * after + other_b).astype(BF16)
    gk[...] = (gk_acc[...] + tail_b[...] * dot(v[...], after, NT)).astype(BF16)
    gv[...] = (gv_acc[...] + tail_b[...] * dot(k[...], after, NN)).astype(BF16)

    swap_copy(0).wait_send()
    swap_copy(1).wait_send()

    def end_ctx(o, c):
        to = lax.rem(me + o, n)
        tot_copy(to, to).wait_send()
        a_copy(to, to).wait_send()
        i_copy(to, to).wait_send()
        return c

    lax.fori_loop(1, n, end_ctx, 0)

    def end_head(o, c):
        to = lax.rem(head + o, m)
        h_copy(to, to).wait_send()
        return c

    lax.fori_loop(1, m, end_head, 0)

    def end_f(to, c):
        f_copy(to, to).wait_send()
        return c

    lax.fori_loop(chip + 1, chips, end_f, 0)

    def end_b(to, c):
        b_copy(to, to).wait_send()
        return c

    lax.fori_loop(0, chip, end_b, 0)


def store(*refs):
    sem = refs[-1]
    copies = [
        pltpu.make_async_copy(refs[i], refs[5 + i], sem.at[i]) for i in range(5)
    ]
    for copy in copies:
        copy.start()
    for copy in copies:
        copy.wait()


def per_device(n, m, query, key, value, gate, decay, gain, state_in, cotangent, regroup):
    rows = query.shape[0]
    chips = n // 2
    nb = rows // T
    piece = rows // n
    big = lambda kind: pltpu.VMEM((rows, T), kind)
    dma = pltpu.SemaphoreType.DMA
    hbm = pl.BlockSpec(memory_space=pl.ANY)
    any_space = pl.BlockSpec(memory_space=pltpu.HBM)
    vmem = pl.BlockSpec(memory_space=pltpu.VMEM)
    results = pl.pallas_call(
        functools.partial(kernel, n, m, rows),
        out_shape=[jax.ShapeDtypeStruct((rows, T), BF16)] * 5,
        in_specs=[any_space] * 9,
        out_specs=[vmem] * 5,
        scratch_shapes=[big(BF16)] * 5
        + [
            pltpu.VMEM((nb, T), F32), pltpu.VMEM((1, T), F32), pltpu.VMEM((1, T, T), F32),
            pltpu.SMEM((n * n,), jnp.int32),
        ]
        + [big(F32)] * 3
        + [
            pltpu.VMEM((rows, rows), F32),
            pltpu.VMEM((rows, rows), BF16),
            big(F32), big(F32), big(F32), pltpu.VMEM((n, piece, T), BF16), big(BF16), pltpu.VMEM((T, rows), BF16), big(F32), big(F32),
        ]
        + [
            pltpu.VMEM((n, 1, T), F32),
            pltpu.VMEM((2, T, T), F32),
            pltpu.VMEM((2, T, T), F32),
            pltpu.VMEM((T, T), BF16),
            pltpu.VMEM((chips, T, T), BF16),
            pltpu.VMEM((T, T), BF16),
            pltpu.VMEM((chips, T, T), BF16),
            pltpu.VMEM((m, 2 * nb, T), F32),
            pltpu.VMEM((n, piece, T), BF16),
            pltpu.VMEM((n, piece, T), BF16),
            pltpu.VMEM((T, T), BF16),
            pltpu.VMEM((n, nb, T), F32),
            pltpu.VMEM((T // piece, piece, T), F32),
            pltpu.SMEM((n,), jnp.int32),
            pltpu.VMEM((rows, rows), BF16),
            pltpu.VMEM((rows, rows), BF16),
        ]
        + [
            dma((9,)), dma((n,)), dma((n,)), dma((2,)), dma((2,)),
            dma((chips,)), dma((chips,)), dma((chips,)), dma((chips,)),
            dma((m,)), dma((m,)), dma((n,)), dma((n,)), dma((n,)), dma((n,)),
        ],
        compiler_params=pltpu.CompilerParams(
            collective_id=0, has_side_effects=True, vmem_limit_bytes=40 << 20
        ),
        name="layer",
    )(
        *[
            pltpu.with_memory_space_constraint(x, pltpu.HBM)
            for x in (
                query, key, value, gate, cotangent,
                decay.reshape((nb, T)), gain.reshape((1, T)), state_in, regroup,
            )
        ]
    )
    return pl.pallas_call(
        store,
        out_shape=[jax.ShapeDtypeStruct((rows, T), BF16)] * 5,
        in_specs=[hbm] * 5,
        out_specs=[any_space] * 5,
        scratch_shapes=[dma((5,))],
        compiler_params=pltpu.CompilerParams(vmem_limit_bytes=1 << 20),
        name="store",
    )(*results)


def solution(mesh):
    rows = P("ctx", "head")
    in_specs = (rows, rows, rows, rows, rows, P("head"), P("head", None, None), rows, P())
    body = functools.partial(per_device, mesh.shape["ctx"], mesh.shape["head"])
    return jax.shard_map(
        body, mesh=mesh, in_specs=in_specs, out_specs=(rows,) * 5, check_vma=False
    )
```
